128 devices in a mesh: tm: 64 (over z, y, x), row: 2 (over core).
Axes of the slice: x: 4, y: 4, z: 4, core: 2. Of those that a mesh axis runs over, the one named last changes fastest.
Arguments:
- transition: float32 [1024, 1024], P('row'), may hold values from -1 to 1, as said below
- gain_fwd: float32 [1024, 1024], P(None, 'row'), may hold values from -0.01171875 to 0.01171875
- gain_bwd: float32 [1024, 1024], P(None, 'row'), may hold values from -0.01171875 to 0.01171875
- blend: float32 [1024, 1024], P(None, 'row'), may hold values from -0.1875 to 0.1875
- prior_state: float32 [1024], replicated, may hold values from -6 to 6
- final_state: float32 [1024], replicated, may hold values from -6 to 6
- obs_index: int32 [2048, 128], P('tm'), may hold values from 0 to 1023
- obs_visible: int32 [2048, 128], P('tm'), may hold values 0 or 1
- obs_value: float32 [2048, 128], P('tm'), may hold values from -6 to 6
Outputs:
- smoothed: float32 [2048, 1024], P('tm', 'row')
The draws below stay inside these ranges and needn't reach their ends.
Inputs may be any that keep to these rules, and one draw needn't show every extreme that they name: `transition`: symmetric; every eigenvalue lies strictly between 0 and 1.
All inputs are finite; a program needn't handle non-finite values. No bound on the sum of `obs_visible` on one device may be relied on, other than what follows from the above.
Results may differ from the reference program's by a relative error of at most 0.0003.
Values sent between devices are 32-bit elements; how exact they have to be, the bound alone decides.
No kernel may reach another device: no remote copies, remote signals or barrier semaphores. Data moves between devices by JAX's collectives and lax.ppermute only.
A program may use at most 128 MiB of HBM per device.

```python
import jax
import jax.numpy as jnp
from jax import lax

S = 1024
P_OBS = 128
EPOCHS = 2048


def draw_transition(key, part):
    first_key, second_key, third_key, fourth_key = jax.random.split(key, 4)
    basis, _ = jnp.linalg.qr(jax.random.normal(first_key, (S, S), jnp.float32))
    slow_rate = jnp.exp(jax.random.uniform(second_key, (S,), jnp.float32, jnp.log(0.25 / EPOCHS), jnp.log(1.0 / EPOCHS)))
    fast_rate = jnp.exp(jax.random.uniform(third_key, (S,), jnp.float32, jnp.log(1.0 / 32.0), jnp.log(0.5)))
    share = 0.5
    ranking = jax.random.permutation(fourth_key, S)
    chosen = ranking.astype(jnp.float32) < share * S
    factors = jnp.exp(-jnp.where(chosen, slow_rate, fast_rate))
    matrix = jnp.dot(basis * factors[None, :], basis.T, precision=lax.Precision.HIGHEST)
    return 0.5 * (matrix + matrix.T)


def with_ends(values, key, least, largest):
    place = [jax.random.randint(jax.random.fold_in(key, axis), (), 0, length) for axis, length in enumerate(values.shape)]
    main_axis = values.shape.index(max(values.shape))
    next_to = place[:main_axis] + [(place[main_axis] + 1) % values.shape[main_axis]] + place[main_axis + 1:]
    return values.at[tuple(place)].set(least).at[tuple(next_to)].set(largest)


def block_scale(key, dims, cuts, low, high):
    def one(dim, shards_of):
        heights = jax.random.uniform(jax.random.fold_in(jax.random.fold_in(key, 6), dim), (shards_of,), jnp.float32, low / len(cuts), high / len(cuts))
        return jnp.repeat(jnp.exp(heights), dims[dim] // shards_of).reshape((-1,) + (1,) * (len(dims) - dim - 1))

    level = one(*cuts[0])
    for cut in cuts[1:]:
        level = level * one(*cut)
    return level


def noise(rng, extent, spread, bound, cuts=(), held_as=jnp.bfloat16):
    loudness = block_scale(rng, extent, cuts, -0.22, 0.18) if cuts else 1.0
    values = jax.random.normal(rng, extent, jnp.float32) * spread * loudness
    return jnp.minimum(jnp.maximum(values, -bound), bound).astype(held_as)


def setup_inputs(seed: int = 0) -> dict:
    keys = jax.random.split(jax.random.key(seed), 10)
    return {
        "transition": draw_transition(jax.random.fold_in(keys[9], 71), 0),
        "gain_fwd": noise(keys[1], (S, S), (EPOCHS * P_OBS) ** -0.5, 0.01171875, ((1, 2),), jnp.float32),
        "gain_bwd": noise(keys[2], (S, S), (EPOCHS * P_OBS) ** -0.5, 0.01171875, ((1, 2),), jnp.float32),
        "blend": noise(keys[3], (S, S), S ** -0.5, 0.1875, ((1, 2),), jnp.float32),
        "prior_state": noise(keys[4], (S,), 1.0, 6.0, (), jnp.float32),
        "final_state": noise(keys[5], (S,), 1.0, 6.0, (), jnp.float32),
        "obs_index": with_ends(jax.random.randint(keys[6], (EPOCHS, P_OBS), 0, S), jax.random.fold_in(keys[6], 1), 0, S - 1).astype(jnp.int32),
        "obs_visible": with_ends((jax.random.randint(keys[7], (EPOCHS, P_OBS), 0, 4) < 3).astype(jnp.int32), jax.random.fold_in(keys[7], 1), 0, 1),
        "obs_value": noise(keys[8], (EPOCHS, P_OBS), 1.0, 6.0, ((0, 64),), jnp.float32),
    }


def reference(transition, gain_fwd, gain_bwd, blend, prior_state, final_state, obs_index, obs_visible, obs_value):
    highest = lax.Precision.HIGHEST
    weights = obs_value * obs_visible.astype(jnp.float32)
    places = jnp.broadcast_to(jnp.arange(EPOCHS, dtype=jnp.int32)[:, None], obs_index.shape)
    sparse = jnp.zeros((EPOCHS, S), jnp.float32).at[places, obs_index].add(weights)
    innov_fwd = jnp.dot(sparse, gain_fwd, precision=highest)
    innov_bwd = jnp.dot(sparse, gain_bwd, precision=highest)

    def advance(state_now, innovation):
        nxt = jnp.dot(transition, state_now, precision=highest) + innovation
        return (nxt, nxt)
    _, seq_fwd = lax.scan(advance, prior_state, innov_fwd)
    _, seq_back = lax.scan(advance, final_state, innov_bwd[::-1])
    seq_bwd = seq_back[::-1]
    return seq_fwd + jnp.dot(seq_bwd - seq_fwd, blend, precision=highest)
```

```python
import jax
import jax.numpy as jnp
from jax import lax
from jax.experimental import pallas as pl
from jax.experimental.pallas import tpu as pltpu
from jax.sharding import PartitionSpec as P

F = jnp.float32
B = jnp.bfloat16
S = 1024
H = 512
Q = 256
EP = 32
PAD = 16


def mm(a, b):
    return lax.dot_general(a, b, (((1,), (0,)), ((), ())), preferred_element_type=F)


def split(x):
    hi = x.astype(B)
    return hi, (x - hi.astype(F)).astype(B)


def product(x, hi, lo):
    n = x.shape[0]
    a, b = split(x)
    p = mm(jnp.concatenate((a, b), axis=0), hi)
    return p[:n] + (p[n:] + mm(a, lo))


def eye(n):
    return lax.broadcasted_iota(jnp.int32, (n, n), 0) == lax.broadcasted_iota(jnp.int32, (n, n), 1)


def low_diagonal(l, i):
    low = l[pl.ds(PAD + i * Q, Q), :].astype(F)
    return jnp.where(eye(Q), jnp.sum(low * low, axis=1, keepdims=True), 0.0)


def square(src, emit, carried, after=None):
    h, l, f = src
    for j in (3, 2, 1, 0):
        cols = pl.ds(j * Q, Q)
        hc = h[pl.ds(PAD, S), cols]
        lc = l[pl.ds(PAD, S), cols]
        for i in range(j + 1):
            rows = pl.ds(0, PAD + Q) if i == 0 and carried is not None else pl.ds(PAD + i * Q, Q)
            p = mm(h[rows, :], hc) + (mm(l[rows, :], hc) + mm(h[rows, :], lc))
            if i == 0 and carried is not None:
                carried[:, cols] = p[:PAD]
                p = p[PAD:]
            if i == j:
                p = p + low_diagonal(l, i)
            at = pl.ds(PAD + i * Q, Q)
            twice = f[pl.ds(i * Q, Q), cols] if f is not None else h[at, cols].astype(F) + l[at, cols].astype(F)
            emit(i, j, 2.0 * twice - p)
        if after is not None:
            after(j)


def put(dst):
    h, l, f = dst

    def one(i, j, d):
        if f is not None:
            f[pl.ds(i * Q, Q), pl.ds(j * Q, Q)] = d
        a, b = split(d)
        h[pl.ds(PAD + i * Q, Q), pl.ds(j * Q, Q)] = a
        l[pl.ds(PAD + i * Q, Q), pl.ds(j * Q, Q)] = b

    def both(i, j, d):
        one(i, j, d)
        if i < j:
            one(j, i, d.T)

    return both


def innovation_kernel(idx, vis, val, gf, gb, keep, send, sparse, both, gain, sem):
    r = lax.axis_index("row")
    copies = [pltpu.make_async_copy(g, gain.at[n], sem.at[n]) for n, g in enumerate((gf, gb))]
    for c in copies:
        c.start()
    low = lax.broadcasted_iota(jnp.int32, (128, 128), 0)
    high = lax.broadcasted_iota(jnp.int32, (8, 128), 0)
    for k in range(EP):
        at = idx[pl.ds(k, 1), :]
        w = val[pl.ds(k, 1), :] * vis[pl.ds(k, 1), :].astype(F)
        place = jnp.where((at & 127) == low, 1.0, 0.0).astype(B)
        part = jnp.where((at >> 7) == high, w, 0.0)
        a, b = split(part)
        rows = lax.dot_general(
            jnp.concatenate((a, b), axis=0), place, (((1,), (1,)), ((), ())), preferred_element_type=F
        )
        rows = rows[:8] + rows[8:]
        for q in range(8):
            sparse[pl.ds(k, 1), pl.ds(q * 128, 128)] = rows[q : q + 1]
    x = sparse[...]
    for n in range(2):
        copies[n].wait()
        both[n] = product(x, *split(gain[n]))

    @pl.when(r == 0)
    def _():
        keep[...] = both[0]
        for k in range(EP):
            send[pl.ds(EP - 1 - k, 1), :] = both[1, pl.ds(k, 1), :]

    @pl.when(r == 1)
    def _():
        send[...] = both[0]
        for k in range(EP):
            keep[pl.ds(EP - 1 - k, 1), :] = both[1, pl.ds(k, 1), :]


HBM = pl.BlockSpec(memory_space=pltpu.HBM)
VMEM = pl.BlockSpec(memory_space=pltpu.VMEM)


def innovation(idx, vis, val, gf, gb):
    half = jax.ShapeDtypeStruct((EP, H), F)
    return pl.pallas_call(
        innovation_kernel,
        out_shape=(half, half),
        in_specs=[VMEM, VMEM, VMEM, HBM, HBM],
        scratch_shapes=[
            pltpu.VMEM((EP, S), F),
            pltpu.VMEM((2, EP, H), F),
            pltpu.VMEM((2, S, H), F),
            pltpu.SemaphoreType.DMA((2,)),
        ],
        compiler_params=pltpu.CompilerParams(vmem_limit_bytes=62 << 20),
        name="innovation",
    )(idx, vis, val, gf, gb)


def ladder_kernel(own, recv, keep, other, ends, kh, kl, ah, al, af, ch, cl, cf, vec, vd, sem):
    r = lax.axis_index("row")
    one = jnp.where(eye(H), 1.0, 0.0)

    def fill(diag, off):
        lower = -off
        for (i, j), d in (((0, 0), one - diag), ((0, 1), lower), ((1, 0), lower.T), ((1, 1), one - recv[...])):
            a, b = split(d)
            af[pl.ds(i * H, H), pl.ds(j * H, H)] = d
            ah[pl.ds(PAD + i * H, H), pl.ds(j * H, H)] = a
            al[pl.ds(PAD + i * H, H), pl.ds(j * H, H)] = b

    @pl.when(r == 0)
    def _():
        fill(own[:, :H], own[:, H:])

    @pl.when(r == 1)
    def _():
        fill(own[:, H:], own[:, :H])

    vec[:, :H] = keep[...]
    vec[:, H:] = other[...]
    at = lax.broadcasted_iota(jnp.int32, (EP, EP), 0)
    at = 2 * (at & 15) + (at >> 4)
    parity = jnp.where(at == lax.broadcasted_iota(jnp.int32, (EP, EP), 1), 1.0, 0.0)

    def save(h, l, slot):
        copies = (
            pltpu.make_async_copy(h.at[pl.ds(PAD, S), :], kh.at[slot], sem.at[0]),
            pltpu.make_async_copy(l.at[pl.ds(PAD, S), :], kl.at[slot], sem.at[1]),
        )
        for c in copies:
            c.start()
        return copies

    def level(src, dst, slot):
        copies = save(src[0], src[1], slot)
        halves = jnp.dot(parity, vec[...], precision=lax.Precision.HIGHEST, preferred_element_type=F)
        even, odd = halves[:PAD], halves[PAD:]
        a, b = split(even)
        src[0][pl.ds(0, PAD), :] = a
        src[1][pl.ds(0, PAD), :] = b
        square(src, put(dst), vd)
        vec[pl.ds(0, PAD), :] = odd + (even - vd[...])
        for c in copies:
            c.wait()

    first, second = (ah, al, af), (ch, cl, cf)

    def two(n, _):
        level(first, second, 2 * n)
        level(second, first, 2 * n + 1)
        return 0

    lax.fori_loop(0, 2, two, 0)
    copies = save(ah, al, 4)
    tail = vec[pl.ds(0, PAD), :]
    p = product(tail, ah[pl.ds(PAD, S), :], al[pl.ds(PAD, S), :])
    end = tail[1:2] + (tail[0:1] - p[0:1])
    ends[...] = jnp.broadcast_to(end.reshape(1, 1, S), ends.shape)
    for c in copies:
        c.wait()


def ladder(own, recv, keep, other, segments):
    store = jax.ShapeDtypeStruct((5, S, S), B)
    slab = pltpu.VMEM((PAD + S, S), B)
    full = pltpu.VMEM((S, S), F)
    return pl.pallas_call(
        ladder_kernel,
        out_shape=(jax.ShapeDtypeStruct((segments, 1, S), F), store, store),
        out_specs=(VMEM, HBM, HBM),
        scratch_shapes=[slab, slab, full, slab, slab, full]
        + [pltpu.VMEM((EP, S), F), pltpu.VMEM((PAD, S), F), pltpu.SemaphoreType.DMA((2,))],
        compiler_params=pltpu.CompilerParams(vmem_limit_bytes=58 << 20),
        name="ladder",
    )(own, recv, keep, other)


def middle_kernel(kh, kl, mh, ml, ah, al, ch, cl, cf, eh, el, sem):
    loads = (
        pltpu.make_async_copy(kh.at[4], ah.at[pl.ds(PAD, S), :], sem.at[0]),
        pltpu.make_async_copy(kl.at[4], al.at[pl.ds(PAD, S), :], sem.at[1]),
    )
    for c in loads:
        c.start()
    for c in loads:
        c.wait()

    def saver(h, l, slot):
        out = []

        def save(j):
            at = pl.ds(j * Q, Q)
            for n, (a, b) in enumerate(((h, mh), (l, ml))):
                c = pltpu.make_async_copy(a.at[pl.ds(PAD + j * Q, Q), :], b.at[slot, at, :], sem.at[2 + slot * 8 + n * 4 + j])
                c.start()
                out.append(c)

        return save, out

    save, first = saver(ch, cl, 0)
    square((ah, al, None), put((ch, cl, cf)), None, save)
    save, second = saver(eh, el, 1)
    square((ch, cl, cf), put((eh, el, None)), None, save)
    for c in first + second:
        c.wait()


def middle(kh, kl):
    store = jax.ShapeDtypeStruct((2, S, S), B)
    slab = pltpu.VMEM((PAD + S, S), B)
    return pl.pallas_call(
        middle_kernel,
        out_shape=(store, store),
        in_specs=[HBM, HBM],
        out_specs=(HBM, HBM),
        scratch_shapes=[slab, slab, slab, slab, pltpu.VMEM((S, S), F), slab, slab, pltpu.SemaphoreType.DMA((18,))],
        compiler_params=pltpu.CompilerParams(vmem_limit_bytes=61 << 20),
        name="middle",
    )(kh, kl)


def sweep_kernel(
    got, prior, final, keep, other, kh, kl, mh, ml,
    out, sh, sl, ch, cl, eh, el, mat, rows, vd, state, sem,
):
    r = lax.axis_index("row")
    seg = lax.axis_index("tm")
    segments = got.shape[0]

    def load(n, hs, ls, hd, ld):
        copies = (pltpu.make_async_copy(hs, hd, sem.at[0, n]), pltpu.make_async_copy(ls, ld, sem.at[1, n]))
        for c in copies:
            c.start()
        return copies

    body = pl.ds(PAD, S)
    last = load(6, mh.at[1], ml.at[1], eh.at[body, :], el.at[body, :])
    pair = load(5, mh.at[0], ml.at[0], ch, cl)
    small = [load(n, kh.at[n], kl.at[n], sh.at[n], sl.at[n]) for n in range(5)]
    sign = 2 * r - 1
    before = jnp.where(r == 0, seg, segments - 1 - seg)
    start = jnp.where(r == 0, prior[...], jnp.concatenate((final[:, H:], final[:, :H]), axis=1))

    def order(shape):
        a = lax.broadcasted_iota(jnp.int32, shape, 0)
        t = jnp.where((a & 31) < 16, 2 * (a & 15), 2 * (a & 15) + 1)
        return 2 * t + (a >> 5)

    for n in range(segments):
        rows[pl.ds(n, 1), :] = got[n]
    q = order((64, segments))
    pick = jnp.where(lax.broadcasted_iota(jnp.int32, (64, segments), 1) == seg + sign * (q + 1), 1.0, 0.0)
    terms = jnp.dot(pick, rows[...], precision=lax.Precision.HIGHEST, preferred_element_type=F)
    terms = terms + jnp.where(order((64, 1)) == before, 1.0, 0.0) * start
    near, far = terms[:32], terms[32:]
    for c in last + pair:
        c.wait()
    pairs = near + (far - product(far, ch[...], cl[...]))
    near, far = pairs[:16], pairs[16:]
    a, b = split(far)
    eh[pl.ds(0, PAD), :] = a
    el[pl.ds(0, PAD), :] = b

    def emit(i, j, d):
        m = jnp.where(eye(Q), 1.0, 0.0) - d if i == j else -d
        mat[pl.ds(i * Q, Q), pl.ds(j * Q, Q)] = m
        if i < j:
            mat[pl.ds(j * Q, Q), pl.ds(i * Q, Q)] = m.T

    square((eh, el, None), emit, vd)
    quads = near + (far - vd[...])
    vd[...] = quads
    lane = lax.broadcasted_iota(jnp.int32, (1, 128), 1)
    mat[:, pl.ds(S, 128)] = jnp.concatenate((quads, jnp.zeros((128 - PAD, S), F)), axis=0).T

    def two(u, z):
        s = PAD - 1 - 2 * u
        wide = jnp.concatenate((z, jnp.where(lane == s, 1.0, 0.0)), axis=1)
        col = jnp.sum(mat[...] * wide, axis=1, keepdims=True)
        return vd[pl.ds(s - 1, 1), :] + jnp.sum(mat[:, pl.ds(0, S)] * col, axis=0, keepdims=True)

    z = lax.fori_loop(0, PAD // 2, two, jnp.zeros((1, S), F))
    state[:, :H] = keep[...]
    state[:, H:] = other[...]
    z8 = jnp.broadcast_to(z, (8, S))
    for c in small[0]:
        c.wait()
    head = z8 - product(z8, sh[0], sl[0])
    state[pl.ds(0, 1), :] = state[pl.ds(0, 1), :] + head[0:1]
    for n in range(5):
        step = 1 << n
        if n:
            for c in small[n]:
                c.wait()
        x = state[...]
        moved = x - product(x, sh[n], sl[n])
        state[pl.ds(step, EP - step), :] = x[step:] + moved[: EP - step]

    @pl.when(r == 0)
    def _():
        out[...] = state[...]

    @pl.when(r == 1)
    def _():
        for k in range(EP):
            out[pl.ds(EP - 1 - k, 1), :] = state[pl.ds(k, 1), :]


def sweep(got, prior, final, keep, other, kh, kl, mh, ml):
    slab = pltpu.VMEM((PAD + S, S), B)
    mats = pltpu.VMEM((S, S), B)
    return pl.pallas_call(
        sweep_kernel,
        out_shape=jax.ShapeDtypeStruct((EP, S), F),
        in_specs=[VMEM] * 5 + [HBM] * 4,
        out_specs=VMEM,
        scratch_shapes=[
            pltpu.VMEM((5, S, S), B),
            pltpu.VMEM((5, S, S), B),
            mats,
            mats,
            slab,
            slab,
            pltpu.VMEM((S, S + 128), F),
            pltpu.VMEM((got.shape[0], S), F),
            pltpu.VMEM((PAD, S), F),
            pltpu.VMEM((EP, S), F),
            pltpu.SemaphoreType.DMA((2, 7)),
        ],
        compiler_params=pltpu.CompilerParams(vmem_limit_bytes=60 << 20),
        name="sweep",
    )(got, prior, final, keep, other, kh, kl, mh, ml)


def blend_kernel(mine, theirs, blend, out):
    r = lax.axis_index("row")
    swapped = jnp.concatenate((theirs[:, H:], theirs[:, :H]), axis=1)
    own = mine[...]
    fwd = jnp.where(r == 0, own, swapped)
    bwd = jnp.where(r == 0, swapped, own)
    gap = bwd - fwd
    total = fwd[:, :H]
    for n, place in enumerate((r, 1 - r)):
        hi, lo = split(blend[pl.ds(pl.multiple_of(place * H, H), H), :])
        total = total + product(gap[:, n * H : (n + 1) * H], hi, lo)
    out[...] = total


def blended(mine, theirs, blend):
    return pl.pallas_call(
        blend_kernel,
        out_shape=jax.ShapeDtypeStruct((EP, H), F),
        compiler_params=pltpu.CompilerParams(vmem_limit_bytes=4 << 20),
        name="blended",
    )(mine, theirs, blend)


def per_device(
    transition, gain_fwd, gain_bwd, blend, prior_state, final_state, obs_index, obs_visible, obs_value
):
    r = lax.axis_index("row")
    segments = lax.axis_size("tm")
    swap = [(0, 1), (1, 0)]
    diag = lax.dynamic_slice_in_dim(transition, r * H, H, 1)
    recv = lax.ppermute(diag, "row", swap)
    keep, send = innovation(obs_index, obs_visible, obs_value, gain_fwd, gain_bwd)
    other = lax.ppermute(send, "row", swap)
    ends, kh, kl = ladder(transition, recv, keep, other, segments)
    got = lax.all_to_all(ends, "tm", 0, 0)
    mh, ml = middle(kh, kl)
    states = sweep(got, prior_state.reshape(1, S), final_state.reshape(1, S), keep, other, kh, kl, mh, ml)
    theirs = lax.ppermute(states, "row", swap)
    return blended(states, theirs, blend)


def solution(mesh):
    placed = (
        P("row", None),
        P(None, "row"),
        P(None, "row"),
        P(None, "row"),
        P(),
        P(),
        P("tm", None),
        P("tm", None),
        P("tm", None),
    )
    return jax.shard_map(
        per_device, mesh=mesh, in_specs=placed, out_specs=P("tm", "row"), check_vma=False
    )
```

```python
import jax
import jax.numpy as jnp
from jax import lax
from jax.experimental import pallas as pl
from jax.experimental.pallas import tpu as pltpu
from jax.sharding import PartitionSpec as P

F = jnp.float32
B = jnp.bfloat16
S = 1024
H = 512
Q = 256
EP = 32
PAD = 16


def mm(a, b):
    return lax.dot_general(a, b, (((1,), (0,)), ((), ())), preferred_element_type=F)


def nt(a, b):
    return lax.dot_general(a, b, (((1,), (1,)), ((), ())), preferred_element_type=F)


def split(x):
    hi = x.astype(B)
    return hi, (x - hi.astype(F)).astype(B)


def product(x, hi, lo):
    n = x.shape[0]
    a, b = split(x)
    p = mm(jnp.concatenate((a, b), axis=0), hi)
    return p[:n] + (p[n:] + mm(a, lo))


def eye(n):
    return lax.broadcasted_iota(jnp.int32, (n, n), 0) == lax.broadcasted_iota(jnp.int32, (n, n), 1)


def low_diagonal(l, i):
    low = l[pl.ds(PAD, S), pl.ds(i * Q, Q)].astype(F)
    return jnp.where(eye(Q), jnp.sum(low * low, axis=0, keepdims=True), 0.0)


def square(src, emit, carried, order=(3, 2, 1, 0), before=None, after=None):
    h, l, f = src
    for j in order:
        if before is not None:
            before(j)
        right = pl.ds(PAD + j * Q, Q)
        hc = h[right, :]
        lc = l[right, :]
        cols = pl.ds(j * Q, Q)
        for i in range(j + 1):
            rows = pl.ds(0, PAD + Q) if i == 0 and carried is not None else pl.ds(PAD + i * Q, Q)
            p = nt(h[rows, :], hc) + (nt(l[rows, :], hc) + nt(h[rows, :], lc))
            if i == 0 and carried is not None:
                carried[:, cols] = p[:PAD]
                p = p[PAD:]
            at = pl.ds(PAD + i * Q, Q)
            if i == j:
                low = l[right, :].astype(F) if before is not None else None
                p = p + (low_diagonal(l, i) if low is None else row_diagonal(low))
            twice = f[pl.ds(i * Q, Q), cols] if f is not None else h[at, cols].astype(F) + l[at, cols].astype(F)
            emit(i, j, 2.0 * twice - p)
        if after is not None:
            after(j)


def row_diagonal(low):
    return jnp.where(eye(Q), jnp.sum(low * low, axis=1, keepdims=True), 0.0)


def put(dst):
    h, l, f = dst

    def one(i, j, d):
        if f is not None:
            f[pl.ds(i * Q, Q), pl.ds(j * Q, Q)] = d
        a, b = split(d)
        h[pl.ds(PAD + i * Q, Q), pl.ds(j * Q, Q)] = a
        l[pl.ds(PAD + i * Q, Q), pl.ds(j * Q, Q)] = b

    def both(i, j, d):
        one(i, j, d)
        if i < j:
            one(j, i, d.T)

    return both


def innovation_kernel(slots, gf, gb, keep, send, sparse, both, gain, sem):
    r = lax.axis_index("row")
    copies = [pltpu.make_async_copy(g, gain.at[n], sem.at[n]) for n, g in enumerate((gf, gb))]
    for c in copies:
        c.start()
    low = lax.broadcasted_iota(jnp.int32, (128, 128), 0)
    high = lax.broadcasted_iota(jnp.int32, (8, 128), 0)
    for k in range(EP):
        w = slots[0, pl.ds(k, 1), :]
        at = slots[1, pl.ds(k, 1), :].astype(jnp.int32)
        place = jnp.where((at & 127) == low, 1.0, 0.0).astype(B)
        part = jnp.where((at >> 7) == high, w, 0.0)
        a, b = split(part)
        rows = lax.dot_general(
            jnp.concatenate((a, b), axis=0), place, (((1,), (1,)), ((), ())), preferred_element_type=F
        )
        rows = rows[:8] + rows[8:]
        for q in range(8):
            sparse[pl.ds(k, 1), pl.ds(q * 128, 128)] = rows[q : q + 1]
    x = sparse[...]
    for n in range(2):
        copies[n].wait()
        both[n] = product(x, *split(gain[n]))

    @pl.when(r == 0)
    def _():
        keep[...] = both[0]
        for k in range(EP):
            send[pl.ds(EP - 1 - k, 1), :] = both[1, pl.ds(k, 1), :]

    @pl.when(r == 1)
    def _():
        send[...] = both[0]
        for k in range(EP):
            keep[pl.ds(EP - 1 - k, 1), :] = both[1, pl.ds(k, 1), :]


HBM = pl.BlockSpec(memory_space=pltpu.HBM)
VMEM = pl.BlockSpec(memory_space=pltpu.VMEM)


def innovation(slots, gf, gb):
    half = jax.ShapeDtypeStruct((EP, H), F)
    return pl.pallas_call(
        innovation_kernel,
        out_shape=(half, half),
        in_specs=[VMEM, HBM, HBM],
        scratch_shapes=[
            pltpu.VMEM((EP, S), F),
            pltpu.VMEM((2, EP, H), F),
            pltpu.VMEM((2, S, H), F),
            pltpu.SemaphoreType.DMA((2,)),
        ],
        compiler_params=pltpu.CompilerParams(vmem_limit_bytes=50 << 20),
        name="innovation",
    )(slots, gf, gb)


def ladder_kernel(own, recv, keep, other, ends, store, ah, al, af, ch, cl, cf, vec, vd, sem):
    r = lax.axis_index("row")
    one = jnp.where(eye(H), 1.0, 0.0)

    def fill(diag, off):
        lower = -off
        for (i, j), d in (((0, 0), one - diag), ((0, 1), lower), ((1, 0), lower.T), ((1, 1), one - recv[...])):
            a, b = split(d)
            af[pl.ds(i * H, H), pl.ds(j * H, H)] = d
            ah[pl.ds(PAD + i * H, H), pl.ds(j * H, H)] = a
            al[pl.ds(PAD + i * H, H), pl.ds(j * H, H)] = b

    @pl.when(r == 0)
    def _():
        fill(own[:, :H], own[:, H:])

    @pl.when(r == 1)
    def _():
        fill(own[:, H:], own[:, :H])

    vec[:, :H] = keep[...]
    vec[:, H:] = other[...]
    at = lax.broadcasted_iota(jnp.int32, (EP, EP), 0)
    at = 2 * (at & 15) + (at >> 4)
    parity = jnp.where(at == lax.broadcasted_iota(jnp.int32, (EP, EP), 1), 1.0, 0.0)

    first, second = (ah, al, af), (ch, cl, cf)

    def saves(src, slot, j):
        n = 0 if src is first else 8
        at = pl.ds(j * Q, Q)
        return [
            pltpu.make_async_copy(src[m].at[pl.ds(PAD + j * Q, Q), :], store.at[5 * m + slot, at, :], sem.at[n + m * 4 + j])
            for m in range(2)
        ]

    def start(src, slot, j):
        for c in saves(src, slot, j):
            c.start()

    def finish(src, slot):
        for j in range(4):
            for c in saves(src, slot, j):
                c.wait()

    def level(src, dst, slot):
        halves = jnp.dot(parity, vec[...], precision=lax.Precision.HIGHEST, preferred_element_type=F)
        even, odd = halves[:PAD], halves[PAD:]
        a, b = split(even)
        src[0][pl.ds(0, PAD), :] = a
        src[1][pl.ds(0, PAD), :] = b
        square(src, put(dst), vd, after=lambda j: start(dst, slot, j))
        vec[pl.ds(0, PAD), :] = odd + (even - vd[...])

    for j in range(4):
        start(first, 0, j)

    def two(n, _):
        level(first, second, 2 * n + 1)
        finish(first, 2 * n)
        level(second, first, 2 * n + 2)
        finish(second, 2 * n + 1)
        return 0

    lax.fori_loop(0, 2, two, 0)
    tail = vec[pl.ds(0, PAD), :]
    p = product(tail, ah[pl.ds(PAD, S), :], al[pl.ds(PAD, S), :])
    end = tail[1:2] + (tail[0:1] - p[0:1])
    ends[...] = jnp.broadcast_to(end.reshape(1, 1, S), ends.shape)
    finish(first, 4)


def ladder(own, recv, keep, other, segments):
    store = jax.ShapeDtypeStruct((10, S, S), B)
    slab = pltpu.VMEM((PAD + S, S), B)
    full = pltpu.VMEM((S, S), F)
    return pl.pallas_call(
        ladder_kernel,
        out_shape=(jax.ShapeDtypeStruct((segments, 1, S), F), store),
        out_specs=(VMEM, HBM),
        scratch_shapes=[slab, slab, full, slab, slab, full]
        + [pltpu.VMEM((EP, S), F), pltpu.VMEM((PAD, S), F), pltpu.SemaphoreType.DMA((16,))],
        compiler_params=pltpu.CompilerParams(vmem_limit_bytes=52 << 20),
        name="ladder",
    )(own, recv, keep, other)


def arriving(hs, ls, hd, ld, sem):
    copies = []
    for j in range(4):
        at, to = pl.ds(j * Q, Q), pl.ds(PAD + j * Q, Q)
        copies.append(
            (
                pltpu.make_async_copy(hs.at[at, :], hd.at[to, :], sem.at[0, j]),
                pltpu.make_async_copy(ls.at[at, :], ld.at[to, :], sem.at[1, j]),
            )
        )
        for c in copies[j]:
            c.start()

    def ready(j):
        for c in copies[j]:
            c.wait()

    return ready


def middle_kernel(powers, more, ah, al, ch, cl, cf, eh, el, sem, come):
    ready = arriving(powers.at[4], powers.at[9], ah, al, come)

    def saver(h, l, slot):
        out = []

        def save(j):
            at = pl.ds(j * Q, Q)
            for n, a in enumerate((h, l)):
                c = pltpu.make_async_copy(a.at[pl.ds(PAD + j * Q, Q), :], more.at[2 * n + slot, at, :], sem.at[slot * 8 + n * 4 + j])
                c.start()
                out.append(c)

        return save, out

    square((ah, al, None), put((ch, cl, cf)), None, (0, 1, 2, 3), ready)
    save, first = saver(ch, cl, 0)
    for j in range(4):
        save(j)
    save, second = saver(eh, el, 1)
    square((ch, cl, cf), put((eh, el, None)), None, after=save)
    for c in first + second:
        c.wait()


def middle(powers):
    slab = pltpu.VMEM((PAD + S, S), B)
    return pl.pallas_call(
        middle_kernel,
        out_shape=jax.ShapeDtypeStruct((6, S, S), B),
        in_specs=[HBM],
        out_specs=HBM,
        scratch_shapes=[slab, slab, slab, slab, pltpu.VMEM((S, S), F), slab, slab]
        + [pltpu.SemaphoreType.DMA((16,)), pltpu.SemaphoreType.DMA((2, 4))],
        compiler_params=pltpu.CompilerParams(vmem_limit_bytes=52 << 20),
        name="middle",
    )(powers)


def sweep_kernel(
    got, prior, final, keep, other, powers, more,
    out, sh, sl, ch, cl, eh, el, mat, rows, vd, state, sem, come,
):
    r = lax.axis_index("row")
    seg = lax.axis_index("tm")
    segments = got.shape[0]

    def load(n, hs, ls, hd, ld):
        copies = (pltpu.make_async_copy(hs, hd, sem.at[0, n]), pltpu.make_async_copy(ls, ld, sem.at[1, n]))
        for c in copies:
            c.start()
        return copies

    ready = arriving(more.at[1], more.at[3], eh, el, come)
    loads = {}
    sign = 2 * r - 1
    before = jnp.where(r == 0, seg, segments - 1 - seg)
    start = jnp.where(r == 0, prior[...], jnp.concatenate((final[:, H:], final[:, :H]), axis=1))

    def order(shape):
        a = lax.broadcasted_iota(jnp.int32, shape, 0)
        t = jnp.where((a & 31) < 16, 2 * (a & 15), 2 * (a & 15) + 1)
        return 2 * t + (a >> 5)

    for n in range(segments):
        rows[pl.ds(n, 1), :] = got[n]
    q = order((64, segments))
    pick = jnp.where(lax.broadcasted_iota(jnp.int32, (64, segments), 1) == seg + sign * (q + 1), 1.0, 0.0)
    terms = jnp.dot(pick, rows[...], precision=lax.Precision.HIGHEST, preferred_element_type=F)
    terms = terms + jnp.where(order((64, 1)) == before, 1.0, 0.0) * start
    near, far = terms[:32], terms[32:]

    def emit(i, j, d):
        m = jnp.where(eye(Q), 1.0, 0.0) - d if i == j else -d
        mat[pl.ds(i * Q, Q), pl.ds(j * Q, Q)] = m
        if i < j:
            mat[pl.ds(j * Q, Q), pl.ds(i * Q, Q)] = m.T

    def fetch(n):
        loads[n] = load(n, powers.at[n], powers.at[5 + n], sh.at[n], sl.at[n])

    def before_block(j):
        ready(j)
        if j == 1:
            loads[5] = load(5, more.at[0], more.at[2], ch, cl)
        if j == 3:
            fetch(0)
            fetch(1)

    square((eh, el, None), emit, None, (0, 1, 2, 3), before_block)
    for c in loads[5]:
        c.wait()
    fetch(2)
    fetch(3)
    fetch(4)
    pairs = near + (far - product(far, ch[...], cl[...]))
    near, far = pairs[:16], pairs[16:]
    quads = near + (far - product(far, eh[pl.ds(PAD, S), :], el[pl.ds(PAD, S), :]))
    vd[...] = quads
    lane = lax.broadcasted_iota(jnp.int32, (1, 128), 1)
    mat[:, pl.ds(S, 128)] = jnp.concatenate((quads, jnp.zeros((128 - PAD, S), F)), axis=0).T

    def two(u, z):
        s = PAD - 1 - 2 * u
        wide = jnp.concatenate((z, jnp.where(lane == s, 1.0, 0.0)), axis=1)
        col = jnp.sum(mat[...] * wide, axis=1, keepdims=True)
        return vd[pl.ds(s - 1, 1), :] + jnp.sum(mat[:, pl.ds(0, S)] * col, axis=0, keepdims=True)

    z = lax.fori_loop(0, PAD // 2, two, jnp.zeros((1, S), F))
    state[:, :H] = keep[...]
    state[:, H:] = other[...]
    z8 = jnp.broadcast_to(z, (8, S))
    for c in loads[0]:
        c.wait()
    head = z8 - product(z8, sh[0], sl[0])
    state[pl.ds(0, 1), :] = state[pl.ds(0, 1), :] + head[0:1]
    for n in range(5):
        step = 1 << n
        if n:
            for c in loads[n]:
                c.wait()
        x = state[...]
        moved = x - product(x, sh[n], sl[n])
        state[pl.ds(step, EP - step), :] = x[step:] + moved[: EP - step]

    @pl.when(r == 0)
    def _():
        out[...] = state[...]

    @pl.when(r == 1)
    def _():
        for k in range(EP):
            out[pl.ds(EP - 1 - k, 1), :] = state[pl.ds(k, 1), :]


def sweep(got, prior, final, keep, other, powers, more):
    slab = pltpu.VMEM((PAD + S, S), B)
    mats = pltpu.VMEM((S, S), B)
    return pl.pallas_call(
        sweep_kernel,
        out_shape=jax.ShapeDtypeStruct((EP, S), F),
        in_specs=[VMEM] * 5 + [HBM] * 2,
        out_specs=VMEM,
        scratch_shapes=[
            pltpu.VMEM((5, S, S), B),
            pltpu.VMEM((5, S, S), B),
            mats,
            mats,
            slab,
            slab,
            pltpu.VMEM((S, S + 128), F),
            pltpu.VMEM((got.shape[0], S), F),
            pltpu.VMEM((PAD, S), F),
            pltpu.VMEM((EP, S), F),
            pltpu.SemaphoreType.DMA((2, 7)),
            pltpu.SemaphoreType.DMA((2, 4)),
        ],
        compiler_params=pltpu.CompilerParams(vmem_limit_bytes=52 << 20),
        name="sweep",
    )(got, prior, final, keep, other, powers, more)


def blend_kernel(mine, theirs, blend, out):
    r = lax.axis_index("row")
    swapped = jnp.concatenate((theirs[:, H:], theirs[:, :H]), axis=1)
    own = mine[...]
    fwd = jnp.where(r == 0, own, swapped)
    bwd = jnp.where(r == 0, swapped, own)
    gap = bwd - fwd
    total = fwd[:, :H]
    for n, place in enumerate((r, 1 - r)):
        hi, lo = split(blend[pl.ds(pl.multiple_of(place * H, H), H), :])
        total = total + product(gap[:, n * H : (n + 1) * H], hi, lo)
    out[...] = total


def blended(mine, theirs, blend):
    return pl.pallas_call(
        blend_kernel,
        out_shape=jax.ShapeDtypeStruct((EP, H), F),
        compiler_params=pltpu.CompilerParams(vmem_limit_bytes=4 << 20),
        name="blended",
    )(mine, theirs, blend)


def per_device(
    transition, gain_fwd, gain_bwd, blend, prior_state, final_state, obs_index, obs_visible, obs_value
):
    r = lax.axis_index("row")
    segments = lax.axis_size("tm")
    swap = [(0, 1), (1, 0)]
    diag = lax.dynamic_slice_in_dim(transition, r * H, H, 1)
    recv = lax.ppermute(diag, "row", swap)
    slots = jnp.stack((obs_value * obs_visible.astype(F), obs_index.astype(F)))
    keep, send = innovation(slots, gain_fwd, gain_bwd)
    other = lax.ppermute(send, "row", swap)
    ends, powers = ladder(transition, recv, keep, other, segments)
    got = lax.all_to_all(ends, "tm", 0, 0)
    more = middle(powers)
    states = sweep(got, prior_state.reshape(1, S), final_state.reshape(1, S), keep, other, powers, more)
    theirs = lax.ppermute(states, "row", swap)
    return blended(states, theirs, blend)


def solution(mesh):
    placed = (
        P("row", None),
        P(None, "row"),
        P(None, "row"),
        P(None, "row"),
        P(),
        P(),
        P("tm", None),
        P("tm", None),
        P("tm", None),
    )
    return jax.shard_map(
        per_device, mesh=mesh, in_specs=placed, out_specs=P("tm", "row"), check_vma=False
    )
```

```python
import jax
import jax.numpy as jnp
from jax import lax
from jax.experimental import pallas as pl
from jax.experimental.pallas import tpu as pltpu
from jax.sharding import PartitionSpec as P

F = jnp.float32
B = jnp.bfloat16
S = 1024
H = 512
Q = 256
EP = 32
PAD = 16


def mm(a, b):
    return lax.dot_general(a, b, (((1,), (0,)), ((), ())), preferred_element_type=F)


def nt(a, b):
    return lax.dot_general(a, b, (((1,), (1,)), ((), ())), preferred_element_type=F)


def split(x):
    hi = x.astype(B)
    return hi, (x - hi.astype(F)).astype(B)


def product(x, hi, lo):
    n = x.shape[0]
    a, b = split(x)
    p = mm(jnp.concatenate((a, b), axis=0), hi)
    return p[:n] + (p[n:] + mm(a, lo))


def eye(n):
    return lax.broadcasted_iota(jnp.int32, (n, n), 0) == lax.broadcasted_iota(jnp.int32, (n, n), 1)


def low_diagonal(l, i):
    low = l[pl.ds(PAD, S), pl.ds(i * Q, Q)].astype(F)
    return jnp.where(eye(Q), jnp.sum(low * low, axis=0, keepdims=True), 0.0)


def square(src, emit, carried, order=(3, 2, 1, 0), before=None, after=None):
    h, l, f = src
    for j in order:
        if before is not None:
            before(j)
        right = pl.ds(PAD + j * Q, Q)
        hc = h[right, :]
        lc = l[right, :]
        cols = pl.ds(j * Q, Q)
        for i in range(j + 1):
            rows = pl.ds(0, PAD + Q) if i == 0 and carried is not None else pl.ds(PAD + i * Q, Q)
            p = nt(h[rows, :], hc) + (nt(l[rows, :], hc) + nt(h[rows, :], lc))
            if i == 0 and carried is not None:
                carried[:, cols] = p[:PAD]
                p = p[PAD:]
            at = pl.ds(PAD + i * Q, Q)
            if i == j:
                low = l[right, :].astype(F) if before is not None else None
                p = p + (low_diagonal(l, i) if low is None else row_diagonal(low))
            twice = f[pl.ds(i * Q, Q), cols] if f is not None else h[at, cols].astype(F) + l[at, cols].astype(F)
            emit(i, j, 2.0 * twice - p)
        if after is not None:
            after(j)


def row_diagonal(low):
    return jnp.where(eye(Q), jnp.sum(low * low, axis=1, keepdims=True), 0.0)


def put(dst):
    h, l, f = dst

    def one(i, j, d):
        if f is not None:
            f[pl.ds(i * Q, Q), pl.ds(j * Q, Q)] = d
        a, b = split(d)
        h[pl.ds(PAD + i * Q, Q), pl.ds(j * Q, Q)] = a
        l[pl.ds(PAD + i * Q, Q), pl.ds(j * Q, Q)] = b

    def both(i, j, d):
        one(i, j, d)
        if i < j:
            one(j, i, d.T)

    return both


def innovation_kernel(slots, gf, gb, keep, send, sparse, both, gain, sem):
    r = lax.axis_index("row")
    copies = [pltpu.make_async_copy(g, gain.at[n], sem.at[n]) for n, g in enumerate((gf, gb))]
    for c in copies:
        c.start()
    low = lax.broadcasted_iota(jnp.int32, (128, 128), 0)
    high = lax.broadcasted_iota(jnp.int32, (8, 128), 0)
    for k in range(EP):
        w = slots[0, pl.ds(k, 1), :]
        at = slots[1, pl.ds(k, 1), :].astype(jnp.int32)
        place = jnp.where((at & 127) == low, 1.0, 0.0).astype(B)
        part = jnp.where((at >> 7) == high, w, 0.0)
        a, b = split(part)
        rows = lax.dot_general(
            jnp.concatenate((a, b), axis=0), place, (((1,), (1,)), ((), ())), preferred_element_type=F
        )
        rows = rows[:8] + rows[8:]
        for q in range(8):
            sparse[pl.ds(k, 1), pl.ds(q * 128, 128)] = rows[q : q + 1]
    x = sparse[...]
    for n in range(2):
        copies[n].wait()
        both[n] = product(x, *split(gain[n]))

    @pl.when(r == 0)
    def _():
        keep[...] = both[0]
        for k in range(EP):
            send[pl.ds(EP - 1 - k, 1), :] = both[1, pl.ds(k, 1), :]

    @pl.when(r == 1)
    def _():
        send[...] = both[0]
        for k in range(EP):
            keep[pl.ds(EP - 1 - k, 1), :] = both[1, pl.ds(k, 1), :]


HBM = pl.BlockSpec(memory_space=pltpu.HBM)
VMEM = pl.BlockSpec(memory_space=pltpu.VMEM)


def innovation(slots, gf, gb):
    half = jax.ShapeDtypeStruct((EP, H), F)
    return pl.pallas_call(
        innovation_kernel,
        out_shape=(half, half),
        in_specs=[VMEM, HBM, HBM],
        scratch_shapes=[
            pltpu.VMEM((EP, S), F),
            pltpu.VMEM((2, EP, H), F),
            pltpu.VMEM((2, S, H), F),
            pltpu.SemaphoreType.DMA((2,)),
        ],
        compiler_params=pltpu.CompilerParams(vmem_limit_bytes=50 << 20),
        name="innovation",
    )(slots, gf, gb)


def ladder_kernel(own, recv, keep, other, ends, store, ah, al, af, ch, cl, cf, vec, vd, sem):
    r = lax.axis_index("row")
    one = jnp.where(eye(H), 1.0, 0.0)

    def fill(diag, off):
        lower = -off
        for (i, j), d in (((0, 0), one - diag), ((0, 1), lower), ((1, 0), lower.T), ((1, 1), one - recv[...])):
            a, b = split(d)
            af[pl.ds(i * H, H), pl.ds(j * H, H)] = d
            ah[pl.ds(PAD + i * H, H), pl.ds(j * H, H)] = a
            al[pl.ds(PAD + i * H, H), pl.ds(j * H, H)] = b

    @pl.when(r == 0)
    def _():
        fill(own[:, :H], own[:, H:])

    @pl.when(r == 1)
    def _():
        fill(own[:, H:], own[:, :H])

    vec[:, :H] = keep[...]
    vec[:, H:] = other[...]
    at = lax.broadcasted_iota(jnp.int32, (EP, EP), 0)
    at = 2 * (at & 15) + (at >> 4)
    parity = jnp.where(at == lax.broadcasted_iota(jnp.int32, (EP, EP), 1), 1.0, 0.0)

    first, second = (ah, al, af), (ch, cl, cf)

    def saves(src, slot, j):
        n = 0 if src is first else 8
        at = pl.ds(j * Q, Q)
        return [
            pltpu.make_async_copy(src[m].at[pl.ds(PAD + j * Q, Q), :], store.at[5 * m + slot, at, :], sem.at[n + m * 4 + j])
            for m in range(2)
        ]

    def start(src, slot, j):
        for c in saves(src, slot, j):
            c.start()

    def finish(src, slot):
        for j in range(4):
            for c in saves(src, slot, j):
                c.wait()

    def level(src, dst, slot):
        halves = jnp.dot(parity, vec[...], precision=lax.Precision.HIGHEST, preferred_element_type=F)
        even, odd = halves[:PAD], halves[PAD:]
        a, b = split(even)
        src[0][pl.ds(0, PAD), :] = a
        src[1][pl.ds(0, PAD), :] = b
        square(src, put(dst), vd, after=lambda j: start(dst, slot, j))
        vec[pl.ds(0, PAD), :] = odd + (even - vd[...])

    for j in range(4):
        start(first, 0, j)

    def two(n, _):
        level(first, second, 2 * n + 1)
        finish(first, 2 * n)
        level(second, first, 2 * n + 2)
        finish(second, 2 * n + 1)
        return 0

    lax.fori_loop(0, 2, two, 0)
    tail = vec[pl.ds(0, PAD), :]
    p = product(tail, ah[pl.ds(PAD, S), :], al[pl.ds(PAD, S), :])
    end = tail[1:2] + (tail[0:1] - p[0:1])
    ends[...] = jnp.broadcast_to(end.reshape(1, 1, S), ends.shape)
    finish(first, 4)


def ladder(own, recv, keep, other, segments):
    store = jax.ShapeDtypeStruct((10, S, S), B)
    slab = pltpu.VMEM((PAD + S, S), B)
    full = pltpu.VMEM((S, S), F)
    return pl.pallas_call(
        ladder_kernel,
        out_shape=(jax.ShapeDtypeStruct((segments, 1, S), F), store),
        out_specs=(VMEM, HBM),
        scratch_shapes=[slab, slab, full, slab, slab, full]
        + [pltpu.VMEM((EP, S), F), pltpu.VMEM((PAD, S), F), pltpu.SemaphoreType.DMA((16,))],
        compiler_params=pltpu.CompilerParams(vmem_limit_bytes=40 << 20),
        name="ladder",
    )(own, recv, keep, other)


def arriving(hs, ls, hd, ld, sem):
    copies = []
    for j in range(4):
        at, to = pl.ds(j * Q, Q), pl.ds(PAD + j * Q, Q)
        copies.append(
            (
                pltpu.make_async_copy(hs.at[at, :], hd.at[to, :], sem.at[0, j]),
                pltpu.make_async_copy(ls.at[at, :], ld.at[to, :], sem.at[1, j]),
            )
        )
        for c in copies[j]:
            c.start()

    def ready(j):
        for c in copies[j]:
            c.wait()

    return ready


def middle_kernel(powers, more, ah, al, ch, cl, cf, eh, el, sem, come):
    ready = arriving(powers.at[4], powers.at[9], ah, al, come)

    def saver(h, l, slot):
        out = []

        def save(j):
            at = pl.ds(j * Q, Q)
            for n, a in enumerate((h, l)):
                c = pltpu.make_async_copy(a.at[pl.ds(PAD + j * Q, Q), :], more.at[2 * n + slot, at, :], sem.at[slot * 8 + n * 4 + j])
                c.start()
                out.append(c)

        return save, out

    square((ah, al, None), put((ch, cl, cf)), None, (0, 1, 2, 3), ready)
    save, first = saver(ch, cl, 0)
    for j in range(4):
        save(j)
    save, second = saver(eh, el, 1)
    square((ch, cl, cf), put((eh, el, None)), None, after=save)
    for c in first + second:
        c.wait()


def middle(powers):
    slab = pltpu.VMEM((PAD + S, S), B)
    return pl.pallas_call(
        middle_kernel,
        out_shape=jax.ShapeDtypeStruct((6, S, S), B),
        in_specs=[HBM],
        out_specs=HBM,
        scratch_shapes=[slab, slab, slab, slab, pltpu.VMEM((S, S), F), slab, slab]
        + [pltpu.SemaphoreType.DMA((16,)), pltpu.SemaphoreType.DMA((2, 4))],
        compiler_params=pltpu.CompilerParams(vmem_limit_bytes=52 << 20),
        name="middle",
    )(powers)


def sweep_kernel(
    got, prior, final, keep, other, powers, more,
    out, sh, sl, ch, cl, eh, el, mat, rows, vd, state, sem, come,
):
    r = lax.axis_index("row")
    seg = lax.axis_index("tm")
    segments = got.shape[0]

    def load(n, hs, ls, hd, ld):
        copies = (pltpu.make_async_copy(hs, hd, sem.at[0, n]), pltpu.make_async_copy(ls, ld, sem.at[1, n]))
        for c in copies:
            c.start()
        return copies

    ready = arriving(more.at[1], more.at[3], eh, el, come)
    loads = {}
    sign = 2 * r - 1
    before = jnp.where(r == 0, seg, segments - 1 - seg)
    start = jnp.where(r == 0, prior[...], jnp.concatenate((final[:, H:], final[:, :H]), axis=1))

    def order(shape):
        a = lax.broadcasted_iota(jnp.int32, shape, 0)
        t = jnp.where((a & 31) < 16, 2 * (a & 15), 2 * (a & 15) + 1)
        return 2 * t + (a >> 5)

    for n in range(segments):
        rows[pl.ds(n, 1), :] = got[n]
    q = order((64, segments))
    pick = jnp.where(lax.broadcasted_iota(jnp.int32, (64, segments), 1) == seg + sign * (q + 1), 1.0, 0.0)
    terms = jnp.dot(pick, rows[...], precision=lax.Precision.HIGHEST, preferred_element_type=F)
    terms = terms + jnp.where(order((64, 1)) == before, 1.0, 0.0) * start
    near, far = terms[:32], terms[32:]

    def emit(i, j, d):
        m = jnp.where(eye(Q), 1.0, 0.0) - d if i == j else -d
        mat[pl.ds(i * Q, Q), pl.ds(j * Q, Q)] = m
        if i < j:
            mat[pl.ds(j * Q, Q), pl.ds(i * Q, Q)] = m.T

    def fetch(n):
        loads[n] = load(n, powers.at[n], powers.at[5 + n], sh.at[n], sl.at[n])

    def before_block(j):
        ready(j)
        if j == 1:
            loads[5] = load(5, more.at[0], more.at[2], ch, cl)
        if j == 3:
            fetch(0)
            fetch(1)

    square((eh, el, None), emit, None, (0, 1, 2, 3), before_block)
    for c in loads[5]:
        c.wait()
    fetch(2)
    fetch(3)
    fetch(4)
    pairs = near + (far - product(far, ch[...], cl[...]))
    near, far = pairs[:16], pairs[16:]
    quads = near + (far - product(far, eh[pl.ds(PAD, S), :], el[pl.ds(PAD, S), :]))
    vd[...] = quads
    lane = lax.broadcasted_iota(jnp.int32, (1, 128), 1)
    mat[:, pl.ds(S, 128)] = jnp.concatenate((quads, jnp.zeros((128 - PAD, S), F)), axis=0).T

    def two(u, z):
        s = PAD - 1 - 2 * u
        wide = jnp.concatenate((z, jnp.where(lane == s, 1.0, 0.0)), axis=1)
        col = jnp.sum(mat[...] * wide, axis=1, keepdims=True)
        return vd[pl.ds(s - 1, 1), :] + jnp.sum(mat[:, pl.ds(0, S)] * col, axis=0, keepdims=True)

    z = lax.fori_loop(0, PAD // 2, two, jnp.zeros((1, S), F))
    state[:, :H] = keep[...]
    state[:, H:] = other[...]
    z8 = jnp.broadcast_to(z, (8, S))
    for c in loads[0]:
        c.wait()
    head = z8 - product(z8, sh[0], sl[0])
    state[pl.ds(0, 1), :] = state[pl.ds(0, 1), :] + head[0:1]
    for n in range(5):
        step = 1 << n
        if n:
            for c in loads[n]:
                c.wait()
        x = state[...]
        moved = x - product(x, sh[n], sl[n])
        state[pl.ds(step, EP - step), :] = x[step:] + moved[: EP - step]

    @pl.when(r == 0)
    def _():
        out[...] = state[...]

    @pl.when(r == 1)
    def _():
        for k in range(EP):
            out[pl.ds(EP - 1 - k, 1), :] = state[pl.ds(k, 1), :]


def sweep(got, prior, final, keep, other, powers, more):
    slab = pltpu.VMEM((PAD + S, S), B)
    mats = pltpu.VMEM((S, S), B)
    return pl.pallas_call(
        sweep_kernel,
        out_shape=jax.ShapeDtypeStruct((EP, S), F),
        in_specs=[VMEM] * 5 + [HBM] * 2,
        out_specs=VMEM,
        scratch_shapes=[
            pltpu.VMEM((5, S, S), B),
            pltpu.VMEM((5, S, S), B),
            mats,
            mats,
            slab,
            slab,
            pltpu.VMEM((S, S + 128), F),
            pltpu.VMEM((got.shape[0], S), F),
            pltpu.VMEM((PAD, S), F),
            pltpu.VMEM((EP, S), F),
            pltpu.SemaphoreType.DMA((2, 7)),
            pltpu.SemaphoreType.DMA((2, 4)),
        ],
        compiler_params=pltpu.CompilerParams(vmem_limit_bytes=52 << 20),
        name="sweep",
    )(got, prior, final, keep, other, powers, more)


def blend_kernel(mine, theirs, blend, out):
    r = lax.axis_index("row")
    swapped = jnp.concatenate((theirs[:, H:], theirs[:, :H]), axis=1)
    own = mine[...]
    fwd = jnp.where(r == 0, own, swapped)
    bwd = jnp.where(r == 0, swapped, own)
    gap = bwd - fwd
    total = fwd[:, :H]
    for n, place in enumerate((r, 1 - r)):
        hi, lo = split(blend[pl.ds(pl.multiple_of(place * H, H), H), :])
        total = total + product(gap[:, n * H : (n + 1) * H], hi, lo)
    out[...] = total


def blended(mine, theirs, blend):
    return pl.pallas_call(
        blend_kernel,
        out_shape=jax.ShapeDtypeStruct((EP, H), F),
        compiler_params=pltpu.CompilerParams(vmem_limit_bytes=4 << 20),
        name="blended",
    )(mine, theirs, blend)


def per_device(
    transition, gain_fwd, gain_bwd, blend, prior_state, final_state, obs_index, obs_visible, obs_value
):
    r = lax.axis_index("row")
    segments = lax.axis_size("tm")
    swap = [(0, 1), (1, 0)]
    diag = lax.dynamic_slice_in_dim(transition, r * H, H, 1)
    recv = lax.ppermute(diag, "row", swap)
    slots = jnp.stack((obs_value * obs_visible.astype(F), obs_index.astype(F)))
    keep, send = innovation(slots, gain_fwd, gain_bwd)
    other = lax.ppermute(send, "row", swap)
    ends, powers = ladder(transition, recv, keep, other, segments)
    got = lax.all_to_all(ends, "tm", 0, 0)
    more = middle(powers)
    states = sweep(got, prior_state.reshape(1, S), final_state.reshape(1, S), keep, other, powers, more)
    theirs = lax.ppermute(states, "row", swap)
    return blended(states, theirs, blend)


def solution(mesh):
    placed = (
        P("row", None),
        P(None, "row"),
        P(None, "row"),
        P(None, "row"),
        P(),
        P(),
        P("tm", None),
        P("tm", None),
        P("tm", None),
    )
    return jax.shard_map(
        per_device, mesh=mesh, in_specs=placed, out_specs=P("tm", "row"), check_vma=False
    )
```
